32 devices in a mesh: row: 4 (over y, x), col: 8 (over z, core).
Axes of the slice: x: 2, y: 2, z: 4, core: 2. Of those that a mesh axis runs over, the one named last changes fastest.
Arguments:
- leaf_state_map: bfloat16 [128, 512, 512], P(('row', 'col')), may hold values from -0.1875 to 0.1875
- leaf_input_map: bfloat16 [128, 512, 256], P(('row', 'col')), may hold values from -0.25 to 0.25
- leaf_weight: bfloat16 [128], P(('row', 'col')), may hold values from 0.29882812 to 3
- leaf_count: int32 [32], P(('row', 'col')), may hold values from 1 to 4, as said below
- mid_state_map: bfloat16 [32, 512, 512], P(('row', 'col')), may hold values from -0.1875 to 0.1875
- mid_input_map: bfloat16 [32, 512, 256], P(('row', 'col')), may hold values from -0.25 to 0.25
- mid_weight: float32 [32], P(('row', 'col')), may hold values from 0.3 to 3
- mid_parent: int32 [32], P(('row', 'col')), may hold values from 0 to 1, as said below
- up_state_map: bfloat16 [8, 512, 512], P('row'), may hold values from -0.1875 to 0.1875
- up_input_map: bfloat16 [8, 512, 256], P('row'), may hold values from -0.25 to 0.25
- up_weight: float32 [8], P('row'), may hold values from 0.3 to 3
- root_cov: bfloat16 [512, 512], replicated, as said below
- state_cost: float32 [512], replicated, may hold values from 0.3 to 3
- control_cost: float32 [256], replicated, may hold values from 0.3 to 3
- noise_cov: float32 [512], replicated, may hold values from 0.05 to 0.5
Outputs:
- root_gain: bfloat16 [256, 512], replicated
- root_value: bfloat16 [512, 512], replicated
- up_gain: bfloat16 [8, 256, 512], P('row')
- up_value: bfloat16 [8, 512, 512], P('row')
- up_cov: bfloat16 [8, 512, 512], P('row')
- mid_gain: bfloat16 [32, 256, 512], P(('row', 'col'))
- mid_value: bfloat16 [32, 512, 512], P(('row', 'col'))
- mid_cov: bfloat16 [32, 512, 512], P(('row', 'col'))
- leaf_cov: bfloat16 [128, 512, 512], P(('row', 'col'))
The draws below stay inside these ranges and needn't reach their ends.
Inputs may be any that keep to these rules, and one draw needn't show every extreme that they name: `leaf_count`: the number of live leaves of each section-2 node; some node has 4 in every draw. `mid_parent`: the parent slot of each section-2 node within its row group; every section-1 node has at least one child. `root_cov`: symmetric positive definite.
All inputs are finite; a program needn't handle non-finite values.
Results may differ from the reference program's by a relative error of at most 0.02.
Values may be sent and summed in bfloat16 or wider, within the bound.
No kernel may reach another device: no remote copies, remote signals or barrier semaphores. Data moves between devices by JAX's collectives and lax.ppermute only.
A program may use at most 128 MiB of HBM per device.

```python
import math
import jax
import jax.numpy as jnp
from jax import lax

NX = 512
NU = 256
LEAF_DEV = 4
S1_ROW = 2
MIDS = 32
LEAVES = 128
UPPERS = 8
N_ROW = 4
N_COL = 8


def draw_leaf_count(key, part):
    base_key = jax.random.fold_in(key, 11)
    first_key, second_key, third_key = jax.random.split(base_key, 3)
    single = jax.random.randint(first_key, (MIDS,), 0, 2)
    larger = jax.random.randint(second_key, (MIDS,), 2, LEAF_DEV + 1)
    counts = jnp.where(single == 0, 1, larger)
    busiest = jax.random.randint(third_key, (), 0, MIDS)
    counts = jnp.where(jnp.arange(MIDS) == busiest, LEAF_DEV, counts)
    return counts.astype(jnp.int32)


def draw_mid_parent(key, part):
    base_key = jax.random.fold_in(key, 29)
    column = jnp.arange(MIDS, dtype=jnp.int32) % N_COL
    chosen = jax.random.randint(base_key, (MIDS,), 0, S1_ROW)
    return jnp.where(column < S1_ROW, column, chosen).astype(jnp.int32)


def draw_root_cov(key, part):
    base_key = jax.random.fold_in(key, 7)
    first_key, second_key = jax.random.split(base_key, 2)
    factor = jax.random.normal(first_key, (NX, NX), jnp.float32)
    diagonal = jax.random.uniform(second_key, (NX,), jnp.float32, 0.5, 1.5)
    matrix = 0.5 * jnp.dot(factor, factor.T) / NX + jnp.diag(diagonal)
    return matrix.astype(jnp.bfloat16)


def level_of(rng, extent, cuts, smallest, high):
    level = 1.0
    for position, shards_of in cuts:
        steps = jax.random.uniform(jax.random.fold_in(jax.random.fold_in(rng, 6), position), (shards_of,), jnp.float32, smallest / len(cuts), high / len(cuts))
        level = level * jnp.repeat(jnp.exp(steps), extent[position] // shards_of).reshape((-1,) + (1,) * (len(extent) - 1 - position))
    return level


def centred(rng, shape, scale, most, shards=(), kind=jnp.bfloat16):
    result = scale * jax.random.normal(rng, shape, jnp.float32)
    if shards:
        result = result * level_of(rng, shape, shards, -0.22, 0.18)
    return jnp.clip(result, -most, most).astype(kind)


def setup_inputs(seed: int = 0) -> dict:
    key_list = jax.random.split(jax.random.key(seed), 16)
    return {
        "leaf_state_map": centred(key_list[0], (LEAVES, NX, NX), (2 * NX) ** -0.5, 0.1875, ((0, 32),)),
        "leaf_input_map": centred(key_list[1], (LEAVES, NX, NU), NX ** -0.5, 0.25, ((0, 32),)),
        "leaf_weight": jnp.clip(jnp.exp(math.log(3.0) - 2.306499 * jax.random.uniform(key_list[2], (LEAVES,), jnp.float32) ** level_of(key_list[2], (LEAVES,), ((0, 32),), -0.2, 0.2)), 0.29882812, 3.0).astype(jnp.bfloat16),
        "leaf_count": draw_leaf_count(jax.random.fold_in(key_list[15], 71), 0),
        "mid_state_map": centred(key_list[4], (MIDS, NX, NX), (2 * NX) ** -0.5, 0.1875, ((0, 32),)),
        "mid_input_map": centred(key_list[5], (MIDS, NX, NU), NX ** -0.5, 0.25, ((0, 32),)),
        "mid_weight": jnp.clip(jnp.exp(math.log(3.0) - 2.3025851 * jax.random.uniform(key_list[6], (MIDS,), jnp.float32) ** level_of(key_list[6], (MIDS,), ((0, 32),), -0.2, 0.2)), 0.3, 3.0),
        "mid_parent": draw_mid_parent(jax.random.fold_in(key_list[15], 71), 0),
        "up_state_map": centred(key_list[8], (UPPERS, NX, NX), (2 * NX) ** -0.5, 0.1875, ((0, 4),)),
        "up_input_map": centred(key_list[9], (UPPERS, NX, NU), NX ** -0.5, 0.25, ((0, 4),)),
        "up_weight": jnp.clip(jnp.exp(math.log(3.0) - 2.3025851 * jax.random.uniform(key_list[10], (UPPERS,), jnp.float32) ** level_of(key_list[10], (UPPERS,), ((0, 4),), -0.2, 0.2)), 0.3, 3.0),
        "root_cov": draw_root_cov(jax.random.fold_in(key_list[15], 71), 0),
        "state_cost": jnp.clip(jnp.exp(jax.random.uniform(key_list[12], (NX,), jnp.float32, math.log(0.3), math.log(3.0))), 0.3, 3.0),
        "control_cost": jnp.clip(jnp.exp(jax.random.uniform(key_list[13], (NU,), jnp.float32, math.log(0.3), math.log(3.0))), 0.3, 3.0),
        "noise_cov": jnp.clip(jnp.exp(jax.random.uniform(key_list[14], (NX,), jnp.float32, math.log(0.05), math.log(0.5))), 0.05, 0.5),
    }


exact_mode = lax.Precision.HIGHEST

def contract(joined, applied):
    return lax.dot_general(joined.astype(jnp.float32), applied.astype(jnp.float32), (((0,), (0,)), ((), ())), preferred_element_type=jnp.float32)

def leaf_term(state_map, input_map, state_cost):
    joined = jnp.concatenate([state_map, input_map], axis=1)
    applied = (state_cost[:, None] * joined.astype(jnp.float32)).astype(jnp.bfloat16)
    return contract(joined, applied)

def node_term(value_matrix, state_map, input_map):
    joined = jnp.concatenate([state_map, input_map], axis=1)
    applied = jnp.dot(value_matrix.astype(jnp.float32), joined.astype(jnp.float32), preferred_element_type=jnp.float32).astype(jnp.bfloat16)
    return contract(joined, applied)

def riccati(combined, state_cost, control_cost):
    block_aa = combined[:NX, :NX]
    block_ba = combined[NX:, :NX]
    block_bb = combined[NX:, NX:]
    hessian = block_bb + jnp.diag(control_cost)
    factor = jnp.linalg.cholesky(hessian)
    feedback = -jax.scipy.linalg.cho_solve((factor, True), block_ba)
    value_matrix = jnp.diag(state_cost) + block_aa + jnp.dot(block_ba.T, feedback, precision=exact_mode)
    return (feedback.astype(jnp.bfloat16), value_matrix.astype(jnp.bfloat16))

def propagate(parent_cov, feedback, state_map, input_map, noise_cov):
    closed = (state_map.astype(jnp.float32) + jnp.dot(input_map.astype(jnp.float32), feedback.astype(jnp.float32), preferred_element_type=jnp.float32)).astype(jnp.bfloat16)
    moved_cov = jnp.dot(closed.astype(jnp.float32), parent_cov.astype(jnp.float32), preferred_element_type=jnp.float32).astype(jnp.bfloat16)
    spread = lax.dot_general(moved_cov.astype(jnp.float32), closed.astype(jnp.float32), (((1,), (1,)), ((), ())), preferred_element_type=jnp.float32)
    return (spread + jnp.diag(noise_cov)).astype(jnp.bfloat16)

def reference(leaf_state_map, leaf_input_map, leaf_weight, leaf_count, mid_state_map, mid_input_map, mid_weight, mid_parent, up_state_map, up_input_map, up_weight, root_cov, state_cost, control_cost, noise_cov):
    slot_ids = jnp.arange(LEAF_DEV, dtype=jnp.int32)

    def lower_node(node_inputs):
        states, controls, weights, live_count, node_state, node_input, node_weight = node_inputs
        live_weight = jnp.where(slot_ids < live_count, weights, jnp.zeros_like(weights))

        def add_leaf(running, leaf_index):
            fresh_term = leaf_term(states[leaf_index], controls[leaf_index], state_cost)
            return (running + live_weight[leaf_index] * fresh_term, None)
        child_sum, unused = lax.scan(add_leaf, jnp.zeros((NX + NU, NX + NU), jnp.float32), slot_ids)
        feedback, value_matrix = riccati(child_sum / jnp.sum(live_weight), state_cost, control_cost)
        return (feedback, value_matrix, node_weight * node_term(value_matrix, node_state, node_input))

    def row_step(carry_state, row_inputs):
        states, controls, weights, counts, node_states, node_inputs, node_weights, parents = row_inputs
        row_gains, row_values, row_terms = lax.map(lower_node, (states, controls, weights, counts, node_states, node_inputs, node_weights))
        slot_pick = (parents[:, None] == jnp.arange(S1_ROW, dtype=jnp.int32)[None, :]).astype(jnp.float32)
        slot_sums = jnp.einsum('cs,cij->sij', slot_pick, row_terms, precision=exact_mode)
        slot_weights = jnp.sum(slot_pick * node_weights[:, None], axis=0)
        return (carry_state, (row_gains, row_values, slot_sums / slot_weights[:, None, None]))
    row_inputs = (leaf_state_map.reshape(N_ROW, N_COL, LEAF_DEV, NX, NX), leaf_input_map.reshape(N_ROW, N_COL, LEAF_DEV, NX, NU), leaf_weight.astype(jnp.float32).reshape(N_ROW, N_COL, LEAF_DEV), leaf_count.reshape(N_ROW, N_COL), mid_state_map.reshape(N_ROW, N_COL, NX, NX), mid_input_map.reshape(N_ROW, N_COL, NX, NU), mid_weight.reshape(N_ROW, N_COL), mid_parent.reshape(N_ROW, N_COL))
    scan_end, row_outputs = lax.scan(row_step, jnp.zeros((), jnp.float32), row_inputs)
    mid_gain = row_outputs[0].reshape(MIDS, NU, NX)
    mid_value = row_outputs[1].reshape(MIDS, NX, NX)
    up_totals = row_outputs[2].reshape(UPPERS, NX + NU, NX + NU)

    def upper_node(node_inputs):
        node_total, node_state, node_input, node_weight = node_inputs
        feedback, value_matrix = riccati(node_total, state_cost, control_cost)
        return (feedback, value_matrix, node_weight * node_term(value_matrix, node_state, node_input))
    up_gain, up_value, up_terms = lax.map(upper_node, (up_totals, up_state_map, up_input_map, up_weight))
    root_gain, root_value = riccati(jnp.sum(up_terms, axis=0) / jnp.sum(up_weight), state_cost, control_cost)
    up_cov = lax.map(lambda node_maps: propagate(root_cov, root_gain, node_maps[0], node_maps[1], noise_cov), (up_state_map, up_input_map))
    parent_index = jnp.arange(MIDS, dtype=jnp.int32) // N_COL * S1_ROW + mid_parent

    def mid_down(node_inputs):
        parent_id, node_state, node_input = node_inputs
        return propagate(up_cov[parent_id], up_gain[parent_id], node_state, node_input, noise_cov)
    mid_cov = lax.map(mid_down, (parent_index, mid_state_map, mid_input_map))

    def leaf_down(node_inputs):
        states, controls, live_count, parent_cov, feedback = node_inputs

        def one_leaf(leaf_index):
            leaf_result = propagate(parent_cov, feedback, states[leaf_index], controls[leaf_index], noise_cov)
            return jnp.where(leaf_index < live_count, leaf_result, jnp.zeros_like(leaf_result))
        return lax.map(one_leaf, slot_ids)
    leaf_cov = lax.map(leaf_down, (leaf_state_map.reshape(MIDS, LEAF_DEV, NX, NX), leaf_input_map.reshape(MIDS, LEAF_DEV, NX, NU), leaf_count, mid_cov, mid_gain))
    leaf_cov = leaf_cov.reshape(LEAVES, NX, NX)
    return (root_gain, root_value, up_gain, up_value, up_cov, mid_gain, mid_value, mid_cov, leaf_cov)
```

```python
import functools

import jax
import jax.numpy as jnp
from jax import lax
from jax.experimental import pallas as pl
from jax.experimental.pallas import tpu as pltpu
from jax.sharding import PartitionSpec as P

NX = 512
NU = 256
S1_ROW = 2
T = 128
HT = T // 2
WROWS = 16

f32 = jnp.float32
bf16 = jnp.bfloat16

BB_BLOCKS = ((0, 0), (1, 0), (1, 1))
BA_BLOCKS = tuple((i, j) for i in range(2) for j in range(4))
AA_BLOCKS = tuple((i, j) for i in range(4) for j in range(i + 1))
FIRST = len(BB_BLOCKS) + len(BA_BLOCKS)
SECOND = len(AA_BLOCKS)
ROWS1 = FIRST * HT + WROWS
ROWS2 = SECOND * HT

NN = (((1,), (0,)), ((), ()))
NT = (((1,), (1,)), ((), ()))
TN = (((0,), (0,)), ((), ()))


def dot(a, b, dims=NN):
    return lax.dot_general(a, b, dims, preferred_element_type=f32)


def split(x):
    high = x.astype(bf16)
    return high, (x - high.astype(f32)).astype(bf16)


def dot3(a, b, dims=NN):
    a_high, a_low = split(a)
    b_high, b_low = split(b)
    return dot(a_high, b_high, dims) + (dot(a_high, b_low, dims) + dot(a_low, b_high, dims))


def tree_sum(terms):
    while len(terms) > 1:
        terms = [terms[i] + terms[i + 1] for i in range(0, len(terms), 2)]
    return terms[0]


def row_of(x, k):
    return jnp.broadcast_to(x[k : k + 1, :], (8, T))


def column_of(x, k):
    return jnp.broadcast_to(x[:, k : k + 1], (8, T))


def negative_inverse(blocks):
    count = len(blocks)
    lane = lax.broadcasted_iota(jnp.int32, (8, T), 1)
    sub = lax.broadcasted_iota(jnp.int32, (8, T), 0)

    def pivot(block, first):
        cols = [column_of(block, first + k) for k in range(8)]
        for k in range(8):
            here = sub == k
            inverse = 1.0 / row_of(cols[k], k)
            lead = jnp.where(here, -1.0, cols[k])
            cols = [
                lead * inverse
                if j == k
                else jnp.where(here, 0.0, cols[j]) - lead * (row_of(cols[j], k) * inverse)
                for j in range(8)
            ]
        inside = (lane >= first) & (lane < first + 8)
        rows = jnp.where(inside, jnp.where(lane - first == sub, -1.0, 0.0), block)
        return tree_sum([cols[j] * row_of(rows, j) for j in range(8)])

    def update(block, lead, first):
        inside = (lane >= first) & (lane < first + 8)
        added = tree_sum([column_of(block, first + k) * row_of(lead, k) for k in range(8)])
        return jnp.where(inside, 0.0, block) + added

    blocks = list(blocks)
    waiting = None
    for i in range(count):
        if waiting is not None and i + 1 < count:
            blocks[i + 1] = update(blocks[i + 1], waiting, 8 * (i - 1))
        lead = pivot(blocks[i], 8 * i)
        if i + 1 < count:
            blocks[i + 1] = update(blocks[i + 1], lead, 8 * i)
        for t in range(count):
            if waiting is not None and t not in (i - 1, i, i + 1):
                blocks[t] = update(blocks[t], waiting, 8 * (i - 1))
        blocks[i] = -lead
        waiting = lead
    last = count - 1
    return [
        blocks[t] if t == last else update(blocks[t], waiting, 8 * last) for t in range(count)
    ]


def invert(source, target):
    rows = negative_inverse([source[8 * i : 8 * i + 8, :] for i in range(T // 8)])
    for i, row in enumerate(rows):
        target[8 * i : 8 * i + 8, :] = -row


def diagonal(block, costs_row):
    i = lax.broadcasted_iota(jnp.int32, block.shape, 0)
    j = lax.broadcasted_iota(jnp.int32, block.shape, 1)
    return block + jnp.where(i == j, jnp.broadcast_to(costs_row, block.shape), 0.0)


def riccati(bb, ba, aa, state_cost, control_cost, hess, inv_a, inv_s, gain, value):
    hess[...] = diagonal(bb(0, 0), control_cost[0:1, :])
    invert(hess, inv_a)
    h21 = bb(1, 0)
    first_inv = inv_a[...]
    through = dot3(h21, first_inv)
    through_t = dot3(first_inv, h21, NT)
    hess[...] = diagonal(bb(1, 1), control_cost[1:2, :]) - dot3(through, h21, NT)
    invert(hess, inv_s)
    block_ba = ba()
    top, bottom = block_ba[:T, :], block_ba[T:, :]
    below = dot3(inv_s[...], bottom - dot3(through, top))
    above = dot3(first_inv, top) - dot3(through_t, below)
    feedback = -jnp.concatenate([above, below], axis=0)
    gain[...] = feedback.astype(bf16)
    for half in range(2):
        width = NU * (half + 1)
        rows = dot3(block_ba[:, NU * half : NU * half + NU], feedback[:, :width], TN)
        for bi in range(2):
            i = 2 * half + bi
            for j in range(i + 1):
                item = aa(i, j) + rows[T * bi : T * bi + T, T * j : T * j + T]
                if i == j:
                    item = diagonal(item, state_cost[i : i + 1, :])
                else:
                    value[T * j : T * j + T, T * i : T * i + T] = item.T.astype(bf16)
                value[T * i : T * i + T, T * j : T * j + T] = item.astype(bf16)


def lower_terms(states, inputs, applied):
    return (
        dot(inputs[...], applied[...], TN),
        dot(states[:, NU:], applied[:, :NX], TN),
        dot(states[:, :NU], applied[:, :NU], TN),
    )


def blocks_of(parts):
    b_rows, a_high, a_low = parts
    for n, (i, j) in enumerate(BB_BLOCKS):
        yield 0, n, b_rows[T * i : T * i + T, NX + T * j : NX + T * j + T]
    for n, (i, j) in enumerate(BA_BLOCKS):
        yield 0, len(BB_BLOCKS) + n, b_rows[T * i : T * i + T, T * j : T * j + T]
    for n, (i, j) in enumerate(AA_BLOCKS):
        source = a_low if i < 2 else a_high
        yield 1, n, source[T * (i % 2) : T * (i % 2) + T, T * j : T * j + T]


def pack(parts, scale, weight_rows, out1, out2):
    outs = (out1, out2)
    for chunk, n, block in blocks_of(parts):
        scaled = (scale * block).astype(bf16)
        for h in range(2):
            outs[chunk][h, HT * n : HT * n + HT, :] = scaled[HT * h : HT * h + HT, :]
    for h in range(2):
        out1[h, HT * FIRST :, :] = weight_rows


def spread_weight(weight, place):
    lane = lax.broadcasted_iota(jnp.int32, (WROWS, T), 1)
    sub = lax.broadcasted_iota(jnp.int32, (WROWS, T), 0)
    full = jnp.full((WROWS, T), weight, f32)
    high = full.astype(bf16).astype(f32)
    item = jnp.where(sub == 0, high, jnp.where(sub == 1, full - high, 0.0))
    return jnp.where(lane == place, item, 0.0).astype(bf16)


def unpack(mine1, other1, mine2, other2, which, sums):
    weight = jnp.sum(mine1[HT * FIRST :, :].astype(f32))
    scale = 1.0 / jnp.full((HT, T), weight, f32)
    swap = jnp.full((HT, T), which, jnp.int32) == 1
    for n in range(FIRST + SECOND):
        mine, other = (mine1, other1) if n < FIRST else (mine2, other2)
        at = HT * (n if n < FIRST else n - FIRST)
        a = mine[at : at + HT, :].astype(f32) * scale
        b = other[at : at + HT, :].astype(f32) * scale
        sums[n, :HT, :] = jnp.where(swap, b, a)
        sums[n, HT:, :] = jnp.where(swap, a, b)


def riccati_packed(sums, state_cost, control_cost, scratch, gain, value):
    riccati(
        lambda i, j: sums[BB_BLOCKS.index((i, j))],
        lambda: jnp.concatenate(
            [
                jnp.concatenate([sums[len(BB_BLOCKS) + 4 * i + j] for j in range(4)], axis=1)
                for i in range(2)
            ],
            axis=0,
        ),
        lambda i, j: sums[FIRST + AA_BLOCKS.index((i, j))],
        state_cost,
        control_cost,
        *scratch,
        gain,
        value,
    )


def apply_value(value, states, inputs, applied):
    applied[:, :NX] = dot(value[...], states[...]).astype(bf16)
    applied[:, NX:] = dot(value[...], inputs[...]).astype(bf16)


def lower_kernel(
    scalars, leaf_state, leaf_input, mid_state, mid_input, state_cost, control_cost,
    gain, value, out1, out2,
    cost_cols, applied, acc_b, acc_high, acc_low, hess, inv_a, inv_s,
):
    slot = pl.program_id(0)
    slots = pl.num_programs(0)
    live = scalars[1].astype(jnp.int32)

    @pl.when(slot == 0)
    def _():
        for i in range(NX // T):
            cost_cols[T * i : T * i + T, :] = jnp.broadcast_to(state_cost[i : i + 1, :], (T, T)).T
        acc_b[...] = jnp.zeros_like(acc_b)
        acc_high[...] = jnp.zeros_like(acc_high)
        acc_low[...] = jnp.zeros_like(acc_low)

    @pl.when(slot < live)
    def _():
        weight = scalars[4 + slot]
        cost = cost_cols[...]
        for j in range(NX // T):
            applied[:, T * j : T * j + T] = (
                cost * leaf_state[:, T * j : T * j + T].astype(f32)
            ).astype(bf16)
        for j in range(NU // T):
            applied[:, NX + T * j : NX + T * j + T] = (
                cost * leaf_input[:, T * j : T * j + T].astype(f32)
            ).astype(bf16)
        for acc, part in zip(
            (acc_b, acc_high, acc_low), lower_terms(leaf_state, leaf_input, applied)
        ):
            acc[...] += weight * part

    @pl.when(slot == slots - 1)
    def _():
        total = lax.fori_loop(
            0, live, lambda n, running: running + scalars[4 + n], jnp.float32(0.0)
        )
        mean_b = 1.0 / jnp.full((T, T), total, f32)
        scale = 1.0 / jnp.full((NU, NX), total, f32)
        riccati(
            lambda i, j: acc_b[T * i : T * i + T, NX + T * j : NX + T * j + T] * mean_b,
            lambda: acc_b[:, :NX] * scale,
            lambda i, j: (acc_low if i < 2 else acc_high)[
                T * (i % 2) : T * (i % 2) + T, T * j : T * j + T
            ]
            * mean_b,
            state_cost,
            control_cost,
            hess,
            inv_a,
            inv_s,
            gain,
            value,
        )
        apply_value(value, mid_state, mid_input, applied)
        pack(
            lower_terms(mid_state, mid_input, applied),
            scalars[0],
            spread_weight(scalars[0], scalars[2].astype(jnp.int32)),
            out1,
            out2,
        )


def upper_kernel(
    which, scalars, mine1, other1, mine2, other2, up_state, up_input, state_cost, control_cost,
    gain, value, out1, out2,
    sums, applied, hess, inv_a, inv_s,
):
    unpack(mine1, other1, mine2, other2, which[0], sums)
    riccati_packed(sums, state_cost, control_cost, (hess, inv_a, inv_s), gain, value)
    slot = which[1]
    states = up_state.at[slot]
    inputs = up_input.at[slot]
    apply_value(value, states, inputs, applied)
    pack(
        lower_terms(states, inputs, applied),
        scalars[0],
        spread_weight(scalars[0], which[2]),
        out1,
        out2,
    )


def propagate(parent_cov, gain, states, inputs, noise_cov, closed, moved, target):
    closed[...] = (states[...].astype(f32) + dot(inputs[...], gain[...])).astype(bf16)
    moved[...] = dot(closed[...], parent_cov[...]).astype(bf16)
    for i in range(NX // T):
        rows = dot(moved[T * i : T * i + T, :], closed[...], NT)
        for j in range(NX // T):
            item = rows[:, T * j : T * j + T]
            if i == j:
                item = diagonal(item, noise_cov[i : i + 1, :])
            target[T * i : T * i + T, T * j : T * j + T] = item.astype(bf16)


def root_kernel(
    which, mine1, other1, mine2, other2, state_cost, control_cost, noise_cov, root_cov,
    up_state, up_input, mid_state, mid_input, leaf_state, leaf_input, parent_gain, mid_gain,
    gain, value, up_cov, mid_cov, leaf_cov,
    sums, hess, inv_a, inv_s, closed, moved,
):
    unpack(mine1, other1, mine2, other2, which[0], sums)
    riccati_packed(sums, state_cost, control_cost, (hess, inv_a, inv_s), gain, value)

    for slot in range(up_state.shape[0]):
        propagate(
            root_cov, gain, up_state.at[slot], up_input.at[slot], noise_cov, closed, moved,
            up_cov.at[slot],
        )
    propagate(
        up_cov.at[which[1]], parent_gain, mid_state, mid_input, noise_cov, closed, moved, mid_cov
    )

    @pl.loop(0, leaf_state.shape[0])
    def _(slot):
        @pl.when(slot < which[2])
        def _():
            propagate(
                mid_cov, mid_gain, leaf_state.at[slot], leaf_input.at[slot], noise_cov, closed,
                moved, leaf_cov.at[slot],
            )

        @pl.when(slot >= which[2])
        def _():
            leaf_cov[slot, :, :] = jnp.zeros((NX, NX), bf16)


SMEM = pl.BlockSpec(memory_space=pltpu.SMEM)
VMEM = pl.BlockSpec(memory_space=pltpu.VMEM)
LIMIT = pltpu.CompilerParams(vmem_limit_bytes=56 << 20)


def matrix(*shape, kind=bf16):
    return jax.ShapeDtypeStruct(shape, kind)


SQUARES = [pltpu.VMEM((T, T), f32)] * 3


def local(
    n_row,
    n_col,
    leaf_state_map,
    leaf_input_map,
    leaf_weight,
    leaf_count,
    mid_state_map,
    mid_input_map,
    mid_weight,
    mid_parent,
    up_state_map,
    up_input_map,
    up_weight,
    root_cov,
    state_cost,
    control_cost,
    noise_cov,
):
    slots = leaf_state_map.shape[0]
    row = lax.axis_index("row")
    col = lax.axis_index("col")
    core = col % 2
    depth = col // 2
    state_rows = state_cost.reshape(NX // T, T)
    control_rows = control_cost.reshape(NU // T, T)
    noise_rows = noise_cov.reshape(NX // T, T)
    parent = mid_parent[0]

    scalars = jnp.concatenate(
        [
            mid_weight,
            leaf_count.astype(f32),
            col.astype(f32)[None],
            jnp.zeros((1,), f32),
            leaf_weight.astype(f32),
        ]
    )
    mid_gain, mid_value, first, second = pl.pallas_call(
        lower_kernel,
        grid=(slots,),
        out_shape=(
            matrix(NU, NX),
            matrix(NX, NX),
            matrix(2, ROWS1, T),
            matrix(2, ROWS2, T),
        ),
        in_specs=[
            SMEM,
            pl.BlockSpec((None, NX, NX), lambda n: (n, 0, 0)),
            pl.BlockSpec((None, NX, NU), lambda n: (n, 0, 0)),
            VMEM,
            VMEM,
            VMEM,
            VMEM,
        ],
        out_specs=(VMEM,) * 4,
        scratch_shapes=[
            pltpu.VMEM((NX, T), f32),
            pltpu.VMEM((NX, NX + NU), bf16),
            pltpu.VMEM((NU, NX + NU), f32),
            pltpu.VMEM((NU, NX), f32),
            pltpu.VMEM((NU, NU), f32),
            *SQUARES,
        ],
        compiler_params=LIMIT,
        name="lower",
    )(
        scalars,
        leaf_state_map,
        leaf_input_map,
        mid_state_map[0],
        mid_input_map[0],
        state_rows,
        control_rows,
    )

    def across(x, flip):
        return lax.ppermute(x, "col", [(i, i ^ flip) for i in range(n_col)])

    def select(flag, a, b):
        return jnp.where(flag, a, b)

    zero = jnp.zeros((), bf16)
    half = depth % 2
    other_parent = lax.ppermute(
        parent.astype(f32).reshape(1, 1), "col", [(i, i ^ 1) for i in range(n_col)]
    )[0, 0]
    own_flag = parent == core
    other_flag = other_parent == core.astype(f32)

    def reduce_col(x):
        y = across(x, 1)
        both = select(own_flag, x, zero).astype(f32) + select(other_flag, y, zero).astype(f32)
        both = both.astype(bf16)
        kept = select(half == 0, both[0], both[1])
        sent = select(half == 0, both[1], both[0])
        kept = kept + across(sent, 2)
        flip = 4
        while flip < n_col:
            kept = kept + across(kept, flip)
            flip = flip * 2
        return kept, across(kept, 2)

    first_mine, first_other = reduce_col(first)
    second_mine, second_other = reduce_col(second)

    up_gain_own, up_value_own, first, second = pl.pallas_call(
        upper_kernel,
        out_shape=(
            matrix(NU, NX),
            matrix(NX, NX),
            matrix(2, ROWS1, T),
            matrix(2, ROWS2, T),
        ),
        in_specs=[SMEM, SMEM] + [VMEM] * 8,
        out_specs=(VMEM,) * 4,
        scratch_shapes=[
            pltpu.VMEM((FIRST + SECOND, T, T), f32),
            pltpu.VMEM((NX, NX + NU), bf16),
            *SQUARES,
        ],
        compiler_params=LIMIT,
        name="upper",
    )(
        jnp.stack([half, core, row * 2 + core]).astype(jnp.int32),
        lax.dynamic_slice(up_weight, (core,), (1,)),
        first_mine,
        first_other,
        second_mine,
        second_other,
        up_state_map,
        up_input_map,
        state_rows,
        control_rows,
    )
    up_gain_other = across(up_gain_own, 1)
    up_value_other = across(up_value_own, 1)
    is_low = core == 0
    up_gain = jnp.stack(
        [select(is_low, up_gain_own, up_gain_other), select(is_low, up_gain_other, up_gain_own)]
    )
    up_value = jnp.stack(
        [select(is_low, up_value_own, up_value_other), select(is_low, up_value_other, up_value_own)]
    )
    parent_gain = select(own_flag, up_gain_own, up_gain_other)

    row_bits = n_row.bit_length() - 1

    def along(x, step):
        bits = (step % row_bits, (step + row_bits // 2) % row_bits)
        return lax.ppermute(
            x,
            ("row", "col"),
            [
                (r * n_col + c, (r ^ (1 << bits[c % 2])) * n_col + c)
                for r in range(n_row)
                for c in range(n_col)
            ],
        )

    def reduce_row(x):
        kept = select(is_low, x[0], x[1])
        sent = select(is_low, x[1], x[0])
        kept = kept + across(sent, 1)
        for step in range(row_bits):
            kept = kept + along(kept, step)
        return kept, across(kept, 1)

    first_mine, first_other = reduce_row(first)
    second_mine, second_other = reduce_row(second)

    root_gain, root_value, up_cov, mid_cov, leaf_cov = pl.pallas_call(
        root_kernel,
        out_shape=(
            matrix(NU, NX),
            matrix(NX, NX),
            matrix(S1_ROW, NX, NX),
            matrix(NX, NX),
            matrix(slots, NX, NX),
        ),
        in_specs=[SMEM] + [VMEM] * 16,
        out_specs=(VMEM,) * 5,
        scratch_shapes=[
            pltpu.VMEM((FIRST + SECOND, T, T), f32),
            *SQUARES,
            pltpu.VMEM((NX, NX), bf16),
            pltpu.VMEM((NX, NX), bf16),
        ],
        compiler_params=LIMIT,
        name="root",
    )(
        jnp.stack([core, parent, leaf_count[0]]).astype(jnp.int32),
        first_mine,
        first_other,
        second_mine,
        second_other,
        state_rows,
        control_rows,
        noise_rows,
        root_cov,
        up_state_map,
        up_input_map,
        mid_state_map[0],
        mid_input_map[0],
        leaf_state_map,
        leaf_input_map,
        parent_gain,
        mid_gain,
    )
    return (
        root_gain,
        root_value,
        up_gain,
        up_value,
        up_cov,
        mid_gain[None],
        mid_value[None],
        mid_cov[None],
        leaf_cov,
    )


def solution(mesh):
    both = P(("row", "col"), None, None)
    flat = P(("row", "col"))
    up = P("row", None, None)
    return jax.shard_map(
        functools.partial(local, mesh.shape["row"], mesh.shape["col"]),
        mesh=mesh,
        in_specs=(
            both, both, flat, flat, both, both, flat, flat, up, up, P("row"), P(), P(), P(), P(),
        ),
        out_specs=(P(), P(), up, up, up, both, both, both, both),
        check_vma=False,
    )
```

```python
import functools

import jax
import jax.numpy as jnp
from jax import lax
from jax.experimental import pallas as pl
from jax.experimental.pallas import tpu as pltpu
from jax.sharding import PartitionSpec as P

NX = 512
NU = 256
S1_ROW = 2
T = 128
HT = T // 2
WROWS = 16

f32 = jnp.float32
bf16 = jnp.bfloat16

FIRST = (
    ("bb", 0, 0), ("bb", 1, 0), ("bb", 1, 1), ("ba", 0, 0), ("ba", 0, 1), ("ba", 0, 2), ("ba", 0, 3),
)
SECOND = tuple(("ba", 1, j) for j in range(4)) + tuple(
    ("aa", i, j) for i in range(4) for j in range(i + 1)
)
PLACE = {name: (chunk, n) for chunk, names in enumerate((FIRST, SECOND)) for n, name in enumerate(names)}
ROWS = (len(FIRST) * HT + WROWS, len(SECOND) * HT + WROWS)

NN = (((1,), (0,)), ((), ()))
NT = (((1,), (1,)), ((), ()))
TN = (((0,), (0,)), ((), ()))


def dot(a, b, dims=NN):
    return lax.dot_general(a, b, dims, preferred_element_type=f32)


def split(x):
    high = x.astype(bf16)
    return high, (x - high.astype(f32)).astype(bf16)


def dot3(a, b, dims=NN):
    a_high, a_low = split(a)
    b_high, b_low = split(b)
    return dot(a_high, b_high, dims) + (dot(a_high, b_low, dims) + dot(a_low, b_high, dims))


def tree_sum(terms):
    while len(terms) > 1:
        terms = [terms[i] + terms[i + 1] for i in range(0, len(terms), 2)]
    return terms[0]


def row_of(x, k):
    return jnp.broadcast_to(x[k : k + 1, :], (8, T))


def column_of(x, k):
    return jnp.take_along_axis(x, jnp.full((8, T), k, jnp.int32), axis=1)


def parts_of(x):
    high = x.astype(bf16).astype(f32)
    rest = x - high
    middle = rest.astype(bf16).astype(f32)
    return high, middle, rest - middle


def negative_inverse(blocks):
    count = len(blocks)
    lane = lax.broadcasted_iota(jnp.int32, (8, T), 1)
    sub = lax.broadcasted_iota(jnp.int32, (8, T), 0)

    def pivot(block, first):
        cols = [column_of(block, first + k) for k in range(8)]
        for k in range(0, 8, 2):
            one, two = sub == k, sub == k + 1
            a = row_of(cols[k], k)
            b = row_of(cols[k + 1], k)
            c = row_of(cols[k + 1], k + 1)
            inverse = 1.0 / (a * c - b * b)
            left = jnp.where(one, -1.0, jnp.where(two, 0.0, cols[k]))
            right = jnp.where(two, -1.0, jnp.where(one, 0.0, cols[k + 1]))
            lead = (c * left - b * right) * inverse
            trail = (a * right - b * left) * inverse
            pair = one | two
            cols = [
                lead
                if j == k
                else trail
                if j == k + 1
                else (jnp.where(pair, 0.0, cols[j]) - lead * row_of(cols[j], k))
                - trail * row_of(cols[j], k + 1)
                for j in range(8)
            ]
        inside = (lane >= first) & (lane < first + 8)
        rows = jnp.where(inside, jnp.where(lane - first == sub, -1.0, 0.0), block)
        return tree_sum([cols[j] * row_of(rows, j) for j in range(8)])

    blocks = list(blocks)
    for i in range(count):
        first = 8 * i
        inside = (lane >= first) & (lane < first + 8)
        raw = blocks[i]
        lead = pivot(raw, first)
        near = [t for t in (i + 1,) if t < count]
        for t in near:
            added = tree_sum([column_of(blocks[t], first + k) * row_of(lead, k) for k in range(8)])
            blocks[t] = jnp.where(inside, 0.0, blocks[t]) + added
        h, m, l = parts_of(raw)
        a, b, c = parts_of(lead)
        far = dot(
            jnp.concatenate([h, h, m, m, h, l], axis=0).astype(bf16),
            jnp.concatenate([a, b, a, b, c, a], axis=0).astype(bf16),
            TN,
        )
        for t in range(count):
            if t != i and t not in near:
                blocks[t] = jnp.where(inside, 0.0, blocks[t]) + far[8 * t : 8 * t + 8, :]
        blocks[i] = -lead
    return blocks


def invert(source, target):
    rows = negative_inverse([source[8 * i : 8 * i + 8, :] for i in range(T // 8)])
    for i, row in enumerate(rows):
        target[8 * i : 8 * i + 8, :] = -row


def diagonal(block, costs_row):
    i = lax.broadcasted_iota(jnp.int32, block.shape, 0)
    j = lax.broadcasted_iota(jnp.int32, block.shape, 1)
    return block + jnp.where(i == j, jnp.broadcast_to(costs_row, block.shape), 0.0)


def eliminate(bb, control_cost, inv_a, through, schur):
    schur[...] = diagonal(bb(0, 0), control_cost[0:1, :])
    invert(schur, inv_a)
    h21 = bb(1, 0)
    through[...] = dot3(h21, inv_a[...])
    schur[...] = diagonal(bb(1, 1), control_cost[1:2, :]) - dot3(through[...], h21, NT)


def finish(block_ba, aa, inv_a, through, inv_s, state_cost, gain, value):
    top, bottom = block_ba[:T, :], block_ba[T:, :]
    below = dot3(inv_s[...], bottom - dot3(through[...], top))
    above = dot3(inv_a[...], top) - dot3(through[...], below, TN)
    feedback = -jnp.concatenate([above, below], axis=0)
    gain[...] = feedback.astype(bf16)
    for half in range(2):
        width = NU * (half + 1)
        rows = dot3(block_ba[:, NU * half : NU * half + NU], feedback[:, :width], TN)
        for bi in range(2):
            i = 2 * half + bi
            for j in range(i + 1):
                item = aa(i, j) + rows[T * bi : T * bi + T, T * j : T * j + T]
                if i == j:
                    item = diagonal(item, state_cost[i : i + 1, :])
                else:
                    value[T * j : T * j + T, T * i : T * i + T] = item.T.astype(bf16)
                value[T * i : T * i + T, T * j : T * j + T] = item.astype(bf16)


def lower_terms(states, inputs, applied):
    return (
        dot(inputs[...], applied[...], TN),
        dot(states[:, NU:], applied[:, :NX], TN),
        dot(states[:, :NU], applied[:, :NU], TN),
    )


def pack(parts, scale, weight_rows, outs):
    b_rows, a_high, a_low = parts
    for (kind, i, j), (chunk, n) in PLACE.items():
        if kind == "aa":
            source = a_low if i < 2 else a_high
            block = source[T * (i % 2) : T * (i % 2) + T, T * j : T * j + T]
        else:
            at = T * j + (NX if kind == "bb" else 0)
            block = b_rows[T * i : T * i + T, at : at + T]
        scaled = (scale * block).astype(bf16)
        for h in range(2):
            outs[chunk][h, HT * n : HT * n + HT, :] = scaled[HT * h : HT * h + HT, :]
    for h in range(2):
        for rows, out in zip(ROWS, outs):
            out[h, rows - WROWS :, :] = weight_rows


def spread_weight(weight, place, tag):
    lane = lax.broadcasted_iota(jnp.int32, (WROWS, T), 1)
    sub = lax.broadcasted_iota(jnp.int32, (WROWS, T), 0)
    full = jnp.full((WROWS, T), weight, f32)
    high = full.astype(bf16).astype(f32)
    item = jnp.where(sub == 0, high, jnp.where(sub == 1, full - high, 0.0))
    item = jnp.where(lane == place, item, 0.0)
    marks = jnp.full((WROWS, T), tag, jnp.int32).astype(f32)
    return jnp.where((sub == 2) & (lane == 0), marks, item).astype(bf16)


def sum_of_rows(rows, first, end):
    sub = lax.broadcasted_iota(jnp.int32, rows.shape, 0)
    return jnp.sum(jnp.where((sub >= first) & (sub < end), rows.astype(f32), 0.0))


def place_in_col():
    col = lax.axis_index("col")
    return col, lax.rem(col, 2), lax.rem(lax.div(col, 2), 2)


def local_sum_kernel(parent, mine, came, kept, sent):
    _, core, half = place_in_col()
    tag = sum_of_rows(came[0, mine.shape[1] - WROWS :, :], 2, 3)
    own = jnp.where(parent[0] == core, 1.0, 0.0)
    other = jnp.where(tag == core.astype(f32), 1.0, 0.0)
    for out, h in ((kept, half), (sent, 1 - half)):
        out[...] = (mine[h].astype(f32) * own + came[h].astype(f32) * other).astype(bf16)


def block_at(chunks, which, scale, name):
    chunk, n = PLACE[name]
    mine, other = chunks[2 * chunk], chunks[2 * chunk + 1]
    a = mine[HT * n : HT * n + HT, :].astype(f32) * scale
    b = other[HT * n : HT * n + HT, :].astype(f32) * scale
    swap = jnp.full((HT, T), which, jnp.int32) == 1
    return jnp.concatenate([jnp.where(swap, b, a), jnp.where(swap, a, b)], axis=0)


def solve_kernel(by_core, mine, other, control_cost, inv_a, through, inv_s, scale, schur):
    _, core, half = place_in_col()
    which = core if by_core else half
    weight = sum_of_rows(mine[ROWS[0] - WROWS :, :], 0, 2)
    scale[...] = 1.0 / jnp.full((HT, T), weight, f32)
    eliminate(
        lambda i, j: block_at((mine, other), which, scale[...], ("bb", i, j)),
        control_cost, inv_a, through, schur,
    )
    invert(schur, inv_s)


def finish_packed(which, chunks, solved, state_cost, gain, value):
    inv_a, through, inv_s, scale = solved

    def at(*name):
        return block_at(chunks, which, scale[...], name)

    block_ba = jnp.concatenate(
        [jnp.concatenate([at("ba", i, j) for j in range(4)], axis=1) for i in range(2)], axis=0
    )
    finish(
        block_ba, lambda i, j: at("aa", i, j), inv_a, through, inv_s, state_cost, gain, value
    )


def apply_value(value, states, inputs, applied):
    applied[:, :NX] = dot(value[...], states[...]).astype(bf16)
    applied[:, NX:] = dot(value[...], inputs[...]).astype(bf16)


def copies(pairs, sems):
    started = [
        pltpu.make_async_copy(source, target, sems.at[n]) for n, (source, target) in enumerate(pairs)
    ]
    for copy in started:
        copy.start()
    return started


def lower_kernel(
    count, mid_weight, parent, leaf_weight, leaf_state_hbm, leaf_input_hbm, mid_state_hbm,
    mid_input_hbm, state_cost, control_cost,
    gain, value, out1, out2,
    leaf_state, leaf_input, mid_state, mid_input, state_sems, input_sems, mid_sems,
    cost_cols, applied, acc_b, acc_high, acc_low, inv_a, through, schur, inv_s,
):
    slots = leaf_state.shape[0]
    live = count[0]
    for n in range(slots):
        pltpu.make_async_copy(leaf_state_hbm.at[n], leaf_state.at[n], state_sems.at[n]).start()
        pltpu.make_async_copy(leaf_input_hbm.at[n], leaf_input.at[n], input_sems.at[n]).start()
    mid_copies = copies(
        ((mid_state_hbm.at[0], mid_state), (mid_input_hbm.at[0], mid_input)), mid_sems
    )
    for i in range(NX // T):
        cost_cols[T * i : T * i + T, :] = jnp.broadcast_to(state_cost[i : i + 1, :], (T, T)).T
    acc_b[...] = jnp.zeros_like(acc_b)
    acc_high[...] = jnp.zeros_like(acc_high)
    acc_low[...] = jnp.zeros_like(acc_low)
    weights = leaf_weight[...].astype(f32)
    places = lax.broadcasted_iota(jnp.int32, weights.shape, 1)

    @pl.loop(0, slots)
    def _(slot):
        states, inputs = leaf_state.at[slot], leaf_input.at[slot]
        pltpu.make_async_copy(leaf_state_hbm.at[slot], states, state_sems.at[slot]).wait()
        pltpu.make_async_copy(leaf_input_hbm.at[slot], inputs, input_sems.at[slot]).wait()

        @pl.when(slot < live)
        def _():
            weight = jnp.sum(jnp.where(places == slot, weights, 0.0))
            cost = cost_cols[...]
            for j in range(NX // T):
                applied[:, T * j : T * j + T] = (
                    cost * states[:, T * j : T * j + T].astype(f32)
                ).astype(bf16)
            for j in range(NU // T):
                applied[:, NX + T * j : NX + T * j + T] = (
                    cost * inputs[:, T * j : T * j + T].astype(f32)
                ).astype(bf16)
            for acc, part in zip(
                (acc_b, acc_high, acc_low), lower_terms(states, inputs, applied)
            ):
                acc[...] += weight * part

    total = jnp.sum(jnp.where(places < live, weights, 0.0))
    mean_b = 1.0 / jnp.full((T, T), total, f32)
    scale = 1.0 / jnp.full((NU, NX), total, f32)
    eliminate(
        lambda i, j: acc_b[T * i : T * i + T, NX + T * j : NX + T * j + T] * mean_b,
        control_cost, inv_a, through, schur,
    )
    invert(schur, inv_s)
    finish(
        acc_b[:, :NX] * scale,
        lambda i, j: (acc_low if i < 2 else acc_high)[
            T * (i % 2) : T * (i % 2) + T, T * j : T * j + T
        ]
        * mean_b,
        inv_a, through, inv_s, state_cost, gain, value,
    )
    for copy in mid_copies:
        copy.wait()
    apply_value(value, mid_state, mid_input, applied)
    pack(
        lower_terms(mid_state, mid_input, applied),
        mid_weight[0],
        spread_weight(mid_weight[0], place_in_col()[0], parent[0]),
        (out1, out2),
    )


def close_kernel(leaf_state, leaf_input, gain, closed):
    closed[...] = (leaf_state[...].astype(f32) + dot(leaf_input[...], gain[...])).astype(bf16)


def upper_kernel(
    up_weight, mine1, other1, mine2, other2, inv_a, through, inv_s, scale,
    up_state_hbm, up_input_hbm, state_cost,
    gain, value, out1, out2,
    up_state, up_input, sems, applied,
):
    _, core, half = place_in_col()
    started = copies(
        ((up_state_hbm.at[core], up_state), (up_input_hbm.at[core], up_input)), sems
    )
    finish_packed(
        half, (mine1, other1, mine2, other2), (inv_a, through, inv_s, scale), state_cost, gain, value
    )
    for copy in started:
        copy.wait()
    apply_value(value, up_state, up_input, applied)
    weight = up_weight[core]
    pack(
        lower_terms(up_state, up_input, applied),
        weight,
        spread_weight(weight, lax.axis_index("row") * S1_ROW + core, core),
        (out1, out2),
    )


def spread(parent_cov, closed, noise_cov, moved, target):
    moved[...] = dot(closed[...], parent_cov[...]).astype(bf16)
    for i in range(NX // T):
        rows = dot(moved[T * i : T * i + T, :], closed[...], NT)
        for j in range(NX // T):
            item = rows[:, T * j : T * j + T]
            if i == j:
                item = diagonal(item, noise_cov[i : i + 1, :])
            target[T * i : T * i + T, T * j : T * j + T] = item.astype(bf16)


def root_kernel(
    count, parent, mine1, other1, mine2, other2, inv_a, through, inv_s, scale,
    state_cost, noise_cov, gain_own, gain_other, value_own, value_other, root_cov_hbm,
    up_state_hbm, up_input_hbm, mid_state_hbm, mid_input_hbm, closed_leaf_hbm,
    gain_out, value_out, up_gain, up_value, up_cov_out, mid_cov_out, leaf_cov_out,
    gain, value, root_cov, up_state, up_input, mid_state, mid_input, closed_leaf, parent_gain,
    up_cov, mid_cov, leaf_cov, closed, moved, in_sems, leaf_sems, out_sems, leaf_out_sems,
):
    _, core, _ = place_in_col()
    slots = closed_leaf.shape[0]
    live = count[0]
    arriving = copies(
        (
            (root_cov_hbm, root_cov),
            (up_state_hbm, up_state),
            (up_input_hbm, up_input),
            (mid_state_hbm.at[0], mid_state),
            (mid_input_hbm.at[0], mid_input),
        ),
        in_sems,
    )
    for n in range(slots):
        pltpu.make_async_copy(closed_leaf_hbm.at[n], closed_leaf.at[n], leaf_sems.at[n]).start()
    leaving = []

    def leave(source, target):
        copy = pltpu.make_async_copy(source, target, out_sems.at[len(leaving)])
        copy.start()
        leaving.append(copy)

    leave(gain_own, up_gain.at[core])
    leave(gain_other, up_gain.at[1 - core])
    leave(value_own, up_value.at[core])
    leave(value_other, up_value.at[1 - core])
    mine_is_parent = jnp.full((NU, NX), parent[0] - core, jnp.int32) == 0
    parent_gain[...] = jnp.where(
        mine_is_parent, gain_own[...].astype(f32), gain_other[...].astype(f32)
    ).astype(bf16)

    finish_packed(
        core, (mine1, other1, mine2, other2), (inv_a, through, inv_s, scale), state_cost, gain, value
    )
    leave(gain, gain_out)
    leave(value, value_out)
    for copy in arriving:
        copy.wait()
    for slot in range(S1_ROW):
        close_kernel(up_state.at[slot], up_input.at[slot], gain, closed)
        spread(root_cov, closed, noise_cov, moved, up_cov.at[slot])
    leave(up_cov, up_cov_out)
    close_kernel(mid_state, mid_input, parent_gain, closed)
    spread(up_cov.at[parent[0]], closed, noise_cov, moved, mid_cov)
    leave(mid_cov, mid_cov_out.at[0])

    @pl.loop(0, slots)
    def _(slot):
        pltpu.make_async_copy(
            closed_leaf_hbm.at[slot], closed_leaf.at[slot], leaf_sems.at[slot]
        ).wait()

        @pl.when(slot < live)
        def _():
            spread(mid_cov, closed_leaf.at[slot], noise_cov, moved, leaf_cov.at[slot])

        @pl.when(slot >= live)
        def _():
            leaf_cov[slot, :, :] = jnp.zeros((NX, NX), bf16)

        pltpu.make_async_copy(
            leaf_cov.at[slot], leaf_cov_out.at[slot], leaf_out_sems.at[slot]
        ).start()

    for copy in leaving:
        copy.wait()

    @pl.loop(0, slots)
    def _(slot):
        pltpu.make_async_copy(
            leaf_cov.at[slot], leaf_cov_out.at[slot], leaf_out_sems.at[slot]
        ).wait()


SMEM = pl.BlockSpec(memory_space=pltpu.SMEM)
VMEM = pl.BlockSpec(memory_space=pltpu.VMEM)
HBM = pl.BlockSpec(memory_space=pltpu.HBM)
DMA = pltpu.SemaphoreType.DMA


def limit(mib):
    return pltpu.CompilerParams(vmem_limit_bytes=mib << 20)


COST = pl.CostEstimate(flops=5 * 10**9, bytes_accessed=1 << 18, transcendentals=0)


def matrix(*shape, kind=bf16):
    return jax.ShapeDtypeStruct(shape, kind)


SQUARES = [pltpu.VMEM((T, T), f32)] * 4
PACKED = tuple(matrix(2, rows, T) for rows in ROWS)


def solve(by_core, chunk, control_rows):
    square = matrix(T, T, kind=f32)
    return pl.pallas_call(
        functools.partial(solve_kernel, by_core),
        out_shape=(square, square, square, matrix(HT, T, kind=f32)),
        in_specs=[VMEM] * 3,
        out_specs=(VMEM,) * 4,
        scratch_shapes=[pltpu.VMEM((T, T), f32)],
        compiler_params=limit(8),
        cost_estimate=COST,
        name="solve",
    )(*chunk, control_rows)


def local(
    n_row,
    n_col,
    leaf_state_map,
    leaf_input_map,
    leaf_weight,
    leaf_count,
    mid_state_map,
    mid_input_map,
    mid_weight,
    mid_parent,
    up_state_map,
    up_input_map,
    up_weight,
    root_cov,
    state_cost,
    control_cost,
    noise_cov,
):
    slots = leaf_state_map.shape[0]
    _, core, _ = place_in_col()
    state_rows = state_cost.reshape(NX // T, T)
    control_rows = control_cost.reshape(NU // T, T)
    noise_rows = noise_cov.reshape(NX // T, T)

    mid_gain, mid_value, *packed = pl.pallas_call(
        lower_kernel,
        out_shape=(matrix(NU, NX), matrix(NX, NX), *PACKED),
        in_specs=[SMEM] * 3 + [VMEM] + [HBM] * 4 + [VMEM] * 2,
        out_specs=(VMEM,) * 4,
        scratch_shapes=[
            pltpu.VMEM((slots, NX, NX), bf16),
            pltpu.VMEM((slots, NX, NU), bf16),
            pltpu.VMEM((NX, NX), bf16),
            pltpu.VMEM((NX, NU), bf16),
            DMA((slots,)),
            DMA((slots,)),
            DMA((2,)),
            pltpu.VMEM((NX, T), f32),
            pltpu.VMEM((NX, NX + NU), bf16),
            pltpu.VMEM((NU, NX + NU), f32),
            pltpu.VMEM((NU, NX), f32),
            pltpu.VMEM((NU, NU), f32),
            *SQUARES,
        ],
        compiler_params=pltpu.CompilerParams(vmem_limit_bytes=67043328),
        name="lower",
    )(
        leaf_count,
        mid_weight,
        mid_parent,
        leaf_weight.reshape(1, slots),
        leaf_state_map,
        leaf_input_map,
        mid_state_map,
        mid_input_map,
        state_rows,
        control_rows,
    )
    def across(x, flip):
        return lax.ppermute(x, "col", [(i, i ^ flip) for i in range(n_col)])

    def local_sum(x):
        part = matrix(*x.shape[1:])
        return pl.pallas_call(
            local_sum_kernel,
            out_shape=(part, part),
            in_specs=[SMEM, VMEM, VMEM],
            out_specs=(VMEM, VMEM),
            compiler_params=limit(8),
            name="local_sum",
        )(mid_parent, x, across(x, 1))

    def rest_of_col(kept):
        flip = 4
        while flip < n_col:
            kept = kept + across(kept, flip)
            flip = flip * 2
        return kept, across(kept, 2)

    (kept1, sent1), (kept2, sent2) = (local_sum(x) for x in packed)
    came1 = across(sent1, 2)
    came1, sent2 = lax.optimization_barrier((came1, sent2))
    came2 = across(sent2, 2)
    came2, gain_then = lax.optimization_barrier((came2, mid_gain))
    closed_leaf = pl.pallas_call(
        close_kernel,
        grid=(slots,),
        out_shape=matrix(slots, NX, NX),
        in_specs=[
            pl.BlockSpec((None, NX, NX), lambda n: (n, 0, 0)),
            pl.BlockSpec((None, NX, NU), lambda n: (n, 0, 0)),
            VMEM,
        ],
        out_specs=pl.BlockSpec((None, NX, NX), lambda n: (n, 0, 0)),
        compiler_params=limit(16),
        cost_estimate=pl.CostEstimate(
            flops=2 * slots * NX * NX * NU, bytes_accessed=slots * NX * 5 * NU * 2, transcendentals=0
        ),
        name="close",
    )(leaf_state_map, leaf_input_map, gain_then)
    first = rest_of_col(kept1 + came1)
    second = rest_of_col(kept2 + came2)
    solved = solve(False, first, control_rows)
    up_weight, closed_leaf = lax.optimization_barrier((up_weight, closed_leaf))

    up_gain_own, up_value_own, *packed = pl.pallas_call(
        upper_kernel,
        out_shape=(matrix(NU, NX), matrix(NX, NX), *PACKED),
        in_specs=[SMEM] + [VMEM] * 8 + [HBM] * 2 + [VMEM],
        out_specs=(VMEM,) * 4,
        scratch_shapes=[
            pltpu.VMEM((NX, NX), bf16),
            pltpu.VMEM((NX, NU), bf16),
            DMA((2,)),
            pltpu.VMEM((NX, NX + NU), bf16),
        ],
        compiler_params=limit(24),
        name="upper",
    )(up_weight, *first, *second, *solved, up_state_map, up_input_map, state_rows)
    up_gain_other = across(up_gain_own, 1)
    up_value_other = across(up_value_own, 1)

    row_bits = n_row.bit_length() - 1
    is_low = core == 0

    def along(x, step):
        bits = (step % row_bits, (step + row_bits // 2) % row_bits)
        return lax.ppermute(
            x,
            ("row", "col"),
            [
                (r * n_col + c, (r ^ (1 << bits[c % 2])) * n_col + c)
                for r in range(n_row)
                for c in range(n_col)
            ],
        )

    def chip_sum(x):
        sent = jnp.where(is_low, x[1], x[0])
        return jnp.where(is_low, x[0], x[1]) + across(sent, 1)

    def rest_of_row(kept):
        for step in range(1, row_bits):
            kept = kept + along(kept, step)
        return kept, across(kept, 1)

    kept1, kept2 = (chip_sum(x) for x in packed)
    came1 = along(kept1, 0)
    came1, kept2 = lax.optimization_barrier((came1, kept2))
    came2 = along(kept2, 0)
    first = rest_of_row(kept1 + came1)
    second = rest_of_row(kept2 + came2)
    solved = solve(True, first, control_rows)

    root_gain, root_value, up_gain, up_value, up_cov, mid_cov, leaf_cov = pl.pallas_call(
        root_kernel,
        out_shape=(
            matrix(NU, NX),
            matrix(NX, NX),
            matrix(S1_ROW, NU, NX),
            matrix(S1_ROW, NX, NX),
            matrix(S1_ROW, NX, NX),
            matrix(1, NX, NX),
            matrix(slots, NX, NX),
        ),
        in_specs=[SMEM] * 2 + [VMEM] * 14 + [HBM] * 6,
        out_specs=(HBM,) * 7,
        scratch_shapes=[
            pltpu.VMEM((NU, NX), bf16),
            pltpu.VMEM((NX, NX), bf16),
            pltpu.VMEM((NX, NX), bf16),
            pltpu.VMEM((S1_ROW, NX, NX), bf16),
            pltpu.VMEM((S1_ROW, NX, NU), bf16),
            pltpu.VMEM((NX, NX), bf16),
            pltpu.VMEM((NX, NU), bf16),
            pltpu.VMEM((slots, NX, NX), bf16),
            pltpu.VMEM((NU, NX), bf16),
            pltpu.VMEM((S1_ROW, NX, NX), bf16),
            pltpu.VMEM((NX, NX), bf16),
            pltpu.VMEM((slots, NX, NX), bf16),
            pltpu.VMEM((NX, NX), bf16),
            pltpu.VMEM((NX, NX), bf16),
            DMA((5,)),
            DMA((slots,)),
            DMA((8,)),
            DMA((slots,)),
        ],
        compiler_params=limit(32),
        name="root",
    )(
        leaf_count,
        mid_parent,
        *first,
        *second,
        *solved,
        state_rows,
        noise_rows,
        up_gain_own,
        up_gain_other,
        up_value_own,
        up_value_other,
        root_cov,
        up_state_map,
        up_input_map,
        mid_state_map,
        mid_input_map,
        closed_leaf,
    )
    return (
        root_gain,
        root_value,
        up_gain,
        up_value,
        up_cov,
        mid_gain[None],
        mid_value[None],
        mid_cov,
        leaf_cov,
    )


def solution(mesh):
    both = P(("row", "col"), None, None)
    flat = P(("row", "col"))
    up = P("row", None, None)
    return jax.shard_map(
        functools.partial(local, mesh.shape["row"], mesh.shape["col"]),
        mesh=mesh,
        in_specs=(
            both, both, flat, flat, both, both, flat, flat, up, up, P("row"), P(), P(), P(), P(),
        ),
        out_specs=(P(), P(), up, up, up, both, both, both, both),
        check_vma=False,
    )
```

```python
import functools

import jax
import jax.numpy as jnp
from jax import lax
from jax.experimental import pallas as pl
from jax.experimental.pallas import tpu as pltpu
from jax.sharding import PartitionSpec as P

NX = 512
NU = 256
S1_ROW = 2
T = 128
HT = T // 2
WROWS = 16

f32 = jnp.float32
bf16 = jnp.bfloat16

FIRST = (("bb", 0, 0), ("bb", 1, 0), ("bb", 1, 1)) + tuple(
    ("ba", i, j) for i in range(2) for j in range(4)
)
SECOND = tuple(("aa", i, j) for i in range(4) for j in range(i + 1))
PLACE = {name: (chunk, n) for chunk, names in enumerate((FIRST, SECOND)) for n, name in enumerate(names)}
ROWS = (len(FIRST) * HT + WROWS, len(SECOND) * HT + WROWS)

NN = (((1,), (0,)), ((), ()))
NT = (((1,), (1,)), ((), ()))
TN = (((0,), (0,)), ((), ()))


def dot(a, b, dims=NN):
    return lax.dot_general(a, b, dims, preferred_element_type=f32)


def split(x):
    high = x.astype(bf16)
    return high, (x - high.astype(f32)).astype(bf16)


def dot3(a, b, dims=NN):
    a_high, a_low = split(a)
    b_high, b_low = split(b)
    return dot(a_high, b_high, dims) + (dot(a_high, b_low, dims) + dot(a_low, b_high, dims))


def tree_sum(terms):
    while len(terms) > 1:
        terms = [terms[i] + terms[i + 1] for i in range(0, len(terms), 2)]
    return terms[0]


def row_of(x, k):
    return jnp.broadcast_to(x[k : k + 1, :], (8, T))


def column_of(x, k):
    return jnp.take_along_axis(x, jnp.full((8, T), k, jnp.int32), axis=1)


def parts_of(x):
    high = x.astype(bf16).astype(f32)
    rest = x - high
    middle = rest.astype(bf16).astype(f32)
    return high, middle, rest - middle


def negative_inverse(blocks):
    count = len(blocks)
    lane = lax.broadcasted_iota(jnp.int32, (8, T), 1)
    sub = lax.broadcasted_iota(jnp.int32, (8, T), 0)

    def pivot(block, first):
        cols = [column_of(block, first + k) for k in range(8)]
        for k in range(0, 8, 2):
            one, two = sub == k, sub == k + 1
            a = row_of(cols[k], k)
            b = row_of(cols[k + 1], k)
            c = row_of(cols[k + 1], k + 1)
            inverse = 1.0 / (a * c - b * b)
            left = jnp.where(one, -1.0, jnp.where(two, 0.0, cols[k]))
            right = jnp.where(two, -1.0, jnp.where(one, 0.0, cols[k + 1]))
            lead = (c * left - b * right) * inverse
            trail = (a * right - b * left) * inverse
            pair = one | two
            cols = [
                lead
                if j == k
                else trail
                if j == k + 1
                else (jnp.where(pair, 0.0, cols[j]) - lead * row_of(cols[j], k))
                - trail * row_of(cols[j], k + 1)
                for j in range(8)
            ]
        inside = (lane >= first) & (lane < first + 8)
        rows = jnp.where(inside, jnp.where(lane - first == sub, -1.0, 0.0), block)
        return tree_sum([cols[j] * row_of(rows, j) for j in range(8)])

    blocks = list(blocks)
    for i in range(count):
        first = 8 * i
        inside = (lane >= first) & (lane < first + 8)
        raw = blocks[i]
        lead = pivot(raw, first)
        near = [t for t in (i + 1,) if t < count]
        for t in near:
            added = tree_sum([column_of(blocks[t], first + k) * row_of(lead, k) for k in range(8)])
            blocks[t] = jnp.where(inside, 0.0, blocks[t]) + added
        h, m, l = parts_of(raw)
        a, b, c = parts_of(lead)
        far = dot(
            jnp.concatenate([h, h, m, m, h, l], axis=0).astype(bf16),
            jnp.concatenate([a, b, a, b, c, a], axis=0).astype(bf16),
            TN,
        )
        for t in range(count):
            if t != i and t not in near:
                blocks[t] = jnp.where(inside, 0.0, blocks[t]) + far[8 * t : 8 * t + 8, :]
        blocks[i] = -lead
    return blocks


def invert(source, target):
    rows = negative_inverse([source[8 * i : 8 * i + 8, :] for i in range(T // 8)])
    for i, row in enumerate(rows):
        target[8 * i : 8 * i + 8, :] = -row


def diagonal(block, costs_row):
    i = lax.broadcasted_iota(jnp.int32, block.shape, 0)
    j = lax.broadcasted_iota(jnp.int32, block.shape, 1)
    return block + jnp.where(i == j, jnp.broadcast_to(costs_row, block.shape), 0.0)


def eliminate(bb, control_cost, inv_a, through, schur):
    schur[...] = diagonal(bb(0, 0), control_cost[0:1, :])
    invert(schur, inv_a)
    h21 = bb(1, 0)
    through[...] = dot3(h21, inv_a[...])
    schur[...] = diagonal(bb(1, 1), control_cost[1:2, :]) - dot3(through[...], h21, NT)


def finish(block_ba, aa, inv_a, through, inv_s, state_cost, gain, value):
    top, bottom = block_ba[:T, :], block_ba[T:, :]
    below = dot3(inv_s[...], bottom - dot3(through[...], top))
    above = dot3(inv_a[...], top) - dot3(through[...], below, TN)
    feedback = -jnp.concatenate([above, below], axis=0)
    gain[...] = feedback.astype(bf16)
    for half in range(2):
        width = NU * (half + 1)
        rows = dot3(block_ba[:, NU * half : NU * half + NU], feedback[:, :width], TN)
        for bi in range(2):
            i = 2 * half + bi
            for j in range(i + 1):
                item = aa(i, j) + rows[T * bi : T * bi + T, T * j : T * j + T]
                if i == j:
                    item = diagonal(item, state_cost[i : i + 1, :])
                else:
                    value[T * j : T * j + T, T * i : T * i + T] = item.T.astype(bf16)
                value[T * i : T * i + T, T * j : T * j + T] = item.astype(bf16)


def lower_terms(states, inputs, applied):
    return (
        dot(inputs[...], applied[...], TN),
        dot(states[:, NU:], applied[:, :NX], TN),
        dot(states[:, :NU], applied[:, :NU], TN),
    )


def pack(parts, scale, weight_rows, outs):
    b_rows, a_high, a_low = parts
    for (kind, i, j), (chunk, n) in PLACE.items():
        if kind == "aa":
            source = a_low if i < 2 else a_high
            block = source[T * (i % 2) : T * (i % 2) + T, T * j : T * j + T]
        else:
            at = T * j + (NX if kind == "bb" else 0)
            block = b_rows[T * i : T * i + T, at : at + T]
        scaled = (scale * block).astype(bf16)
        for h in range(2):
            outs[chunk][h, HT * n : HT * n + HT, :] = scaled[HT * h : HT * h + HT, :]
    for h in range(2):
        for rows, out in zip(ROWS, outs):
            out[h, rows - WROWS :, :] = weight_rows


def spread_weight(weight, place, tag):
    lane = lax.broadcasted_iota(jnp.int32, (WROWS, T), 1)
    sub = lax.broadcasted_iota(jnp.int32, (WROWS, T), 0)
    full = jnp.full((WROWS, T), weight, f32)
    high = full.astype(bf16).astype(f32)
    item = jnp.where(sub == 0, high, jnp.where(sub == 1, full - high, 0.0))
    item = jnp.where(lane == place, item, 0.0)
    marks = jnp.full((WROWS, T), tag, jnp.int32).astype(f32)
    return jnp.where((sub == 2) & (lane == 0), marks, item).astype(bf16)


def sum_of_rows(rows, first, end):
    sub = lax.broadcasted_iota(jnp.int32, rows.shape, 0)
    return jnp.sum(jnp.where((sub >= first) & (sub < end), rows.astype(f32), 0.0))


def place_in_col():
    col = lax.axis_index("col")
    return col, lax.rem(col, 2), lax.rem(lax.div(col, 2), 2)


def local_sum_kernel(parent, mine, came, kept, sent):
    _, core, half = place_in_col()
    tag = sum_of_rows(came[0, mine.shape[1] - WROWS :, :], 2, 3)
    own = jnp.where(parent[0] == core, 1.0, 0.0)
    other = jnp.where(tag == core.astype(f32), 1.0, 0.0)
    for out, h in ((kept, half), (sent, 1 - half)):
        out[...] = (mine[h].astype(f32) * own + came[h].astype(f32) * other).astype(bf16)


def block_at(chunks, which, scale, name):
    chunk, n = PLACE[name]
    mine, other = chunks[2 * chunk], chunks[2 * chunk + 1]
    a = mine[HT * n : HT * n + HT, :].astype(f32) * scale
    b = other[HT * n : HT * n + HT, :].astype(f32) * scale
    swap = jnp.full((HT, T), which, jnp.int32) == 1
    return jnp.concatenate([jnp.where(swap, b, a), jnp.where(swap, a, b)], axis=0)


def solve_kernel(by_core, mine, other, control_cost, inv_a, through, inv_s, scale, schur):
    _, core, half = place_in_col()
    which = core if by_core else half
    weight = sum_of_rows(mine[ROWS[0] - WROWS :, :], 0, 2)
    scale[...] = 1.0 / jnp.full((HT, T), weight, f32)
    eliminate(
        lambda i, j: block_at((mine, other), which, scale[...], ("bb", i, j)),
        control_cost, inv_a, through, schur,
    )
    invert(schur, inv_s)


def finish_packed(which, chunks, solved, state_cost, gain, value):
    inv_a, through, inv_s, scale = solved

    def at(*name):
        return block_at(chunks, which, scale[...], name)

    block_ba = jnp.concatenate(
        [jnp.concatenate([at("ba", i, j) for j in range(4)], axis=1) for i in range(2)], axis=0
    )
    finish(
        block_ba, lambda i, j: at("aa", i, j), inv_a, through, inv_s, state_cost, gain, value
    )


def apply_value(value, states, inputs, applied):
    applied[:, :NX] = dot(value[...], states[...]).astype(bf16)
    applied[:, NX:] = dot(value[...], inputs[...]).astype(bf16)


def copies(pairs, sems):
    started = [
        pltpu.make_async_copy(source, target, sems.at[n]) for n, (source, target) in enumerate(pairs)
    ]
    for copy in started:
        copy.start()
    return started


def lower_kernel(
    count, mid_weight, parent, leaf_weight, leaf_state_hbm, leaf_input_hbm, mid_state_hbm,
    mid_input_hbm, state_cost, control_cost,
    gain, value, out1, out2,
    leaf_state, leaf_input, mid_state, mid_input, state_sems, input_sems, mid_sems,
    cost_cols, applied, acc_b, acc_high, acc_low, inv_a, through, schur, inv_s,
):
    slots = leaf_state.shape[0]
    live = count[0]
    for n in range(slots):
        pltpu.make_async_copy(leaf_state_hbm.at[n], leaf_state.at[n], state_sems.at[n]).start()
        pltpu.make_async_copy(leaf_input_hbm.at[n], leaf_input.at[n], input_sems.at[n]).start()
    mid_copies = copies(
        ((mid_state_hbm.at[0], mid_state), (mid_input_hbm.at[0], mid_input)), mid_sems
    )
    for i in range(NX // T):
        cost_cols[T * i : T * i + T, :] = jnp.broadcast_to(state_cost[i : i + 1, :], (T, T)).T
    acc_b[...] = jnp.zeros_like(acc_b)
    acc_high[...] = jnp.zeros_like(acc_high)
    acc_low[...] = jnp.zeros_like(acc_low)
    weights = leaf_weight[...].astype(f32)
    places = lax.broadcasted_iota(jnp.int32, weights.shape, 1)

    @pl.loop(0, slots)
    def _(slot):
        states, inputs = leaf_state.at[slot], leaf_input.at[slot]
        pltpu.make_async_copy(leaf_state_hbm.at[slot], states, state_sems.at[slot]).wait()
        pltpu.make_async_copy(leaf_input_hbm.at[slot], inputs, input_sems.at[slot]).wait()

        @pl.when(slot < live)
        def _():
            weight = jnp.sum(jnp.where(places == slot, weights, 0.0))
            cost = cost_cols[...]
            for j in range(NX // T):
                applied[:, T * j : T * j + T] = (
                    cost * states[:, T * j : T * j + T].astype(f32)
                ).astype(bf16)
            for j in range(NU // T):
                applied[:, NX + T * j : NX + T * j + T] = (
                    cost * inputs[:, T * j : T * j + T].astype(f32)
                ).astype(bf16)
            for acc, part in zip(
                (acc_b, acc_high, acc_low), lower_terms(states, inputs, applied)
            ):
                acc[...] += weight * part

    total = jnp.sum(jnp.where(places < live, weights, 0.0))
    mean_b = 1.0 / jnp.full((T, T), total, f32)
    scale = 1.0 / jnp.full((NU, NX), total, f32)
    eliminate(
        lambda i, j: acc_b[T * i : T * i + T, NX + T * j : NX + T * j + T] * mean_b,
        control_cost, inv_a, through, schur,
    )
    invert(schur, inv_s)
    finish(
        acc_b[:, :NX] * scale,
        lambda i, j: (acc_low if i < 2 else acc_high)[
            T * (i % 2) : T * (i % 2) + T, T * j : T * j + T
        ]
        * mean_b,
        inv_a, through, inv_s, state_cost, gain, value,
    )
    for copy in mid_copies:
        copy.wait()
    apply_value(value, mid_state, mid_input, applied)
    pack(
        lower_terms(mid_state, mid_input, applied),
        mid_weight[0],
        spread_weight(mid_weight[0], place_in_col()[0], parent[0]),
        (out1, out2),
    )


def close_kernel(leaf_state, leaf_input, gain, closed):
    closed[...] = (leaf_state[...].astype(f32) + dot(leaf_input[...], gain[...])).astype(bf16)


def upper_kernel(
    up_weight, mine1, other1, mine2, other2, inv_a, through, inv_s, scale,
    up_state_hbm, up_input_hbm, state_cost,
    gain, value, out,
    up_state, up_input, sems, applied,
):
    _, core, half = place_in_col()
    started = copies(
        ((up_state_hbm.at[core], up_state), (up_input_hbm.at[core], up_input)), sems
    )
    finish_packed(
        half, (mine1, other1, mine2, other2), (inv_a, through, inv_s, scale), state_cost, gain, value
    )
    for copy in started:
        copy.wait()
    apply_value(value, up_state, up_input, applied)
    weight = up_weight[core]
    pack(
        lower_terms(up_state, up_input, applied),
        weight,
        spread_weight(weight, lax.axis_index("row") * S1_ROW + core, core),
        (out.at[:, : ROWS[0], :], out.at[:, ROWS[0] :, :]),
    )


def spread(parent_cov, closed, noise_cov, moved, target):
    moved[...] = dot(closed[...], parent_cov[...]).astype(bf16)
    for i in range(NX // T):
        rows = dot(moved[T * i : T * i + T, :], closed[...], NT)
        for j in range(NX // T):
            item = rows[:, T * j : T * j + T]
            if i == j:
                item = diagonal(item, noise_cov[i : i + 1, :])
            target[T * i : T * i + T, T * j : T * j + T] = item.astype(bf16)


def root_kernel(
    count, parent, mine, other, state_cost, control_cost, noise_cov, gain_own, gain_other, value_own, value_other, root_cov_hbm,
    up_state_hbm, up_input_hbm, mid_state_hbm, mid_input_hbm, closed_leaf_hbm,
    gain_out, value_out, up_gain, up_value, up_cov_out, mid_cov_out, leaf_cov_out,
    gain, value, root_cov, up_state, up_input, mid_state, mid_input, closed_leaf, parent_gain,
    up_cov, mid_cov, leaf_cov, closed, moved, in_sems, leaf_sems, out_sems, leaf_out_sems,
    inv_a, through, schur, inv_s, scale,
):
    _, core, _ = place_in_col()
    slots = closed_leaf.shape[0]
    live = count[0]
    arriving = copies(
        (
            (root_cov_hbm, root_cov),
            (up_state_hbm, up_state),
            (up_input_hbm, up_input),
            (mid_state_hbm.at[0], mid_state),
            (mid_input_hbm.at[0], mid_input),
        ),
        in_sems,
    )
    for n in range(slots):
        pltpu.make_async_copy(closed_leaf_hbm.at[n], closed_leaf.at[n], leaf_sems.at[n]).start()
    leaving = []

    def leave(source, target):
        copy = pltpu.make_async_copy(source, target, out_sems.at[len(leaving)])
        copy.start()
        leaving.append(copy)

    leave(gain_own, up_gain.at[core])
    leave(gain_other, up_gain.at[1 - core])
    leave(value_own, up_value.at[core])
    leave(value_other, up_value.at[1 - core])
    mine_is_parent = jnp.full((NU, NX), parent[0] - core, jnp.int32) == 0
    parent_gain[...] = jnp.where(
        mine_is_parent, gain_own[...].astype(f32), gain_other[...].astype(f32)
    ).astype(bf16)

    mine1, mine2 = mine.at[: ROWS[0], :], mine.at[ROWS[0] :, :]
    other1, other2 = other.at[: ROWS[0], :], other.at[ROWS[0] :, :]
    solve_kernel(True, mine1, other1, control_cost, inv_a, through, inv_s, scale, schur)
    finish_packed(
        core, (mine1, other1, mine2, other2), (inv_a, through, inv_s, scale), state_cost, gain, value
    )
    leave(gain, gain_out)
    leave(value, value_out)
    for copy in arriving:
        copy.wait()
    for slot in range(S1_ROW):
        close_kernel(up_state.at[slot], up_input.at[slot], gain, closed)
        spread(root_cov, closed, noise_cov, moved, up_cov.at[slot])
    leave(up_cov, up_cov_out)
    close_kernel(mid_state, mid_input, parent_gain, closed)
    spread(up_cov.at[parent[0]], closed, noise_cov, moved, mid_cov)
    leave(mid_cov, mid_cov_out.at[0])

    @pl.loop(0, slots)
    def _(slot):
        pltpu.make_async_copy(
            closed_leaf_hbm.at[slot], closed_leaf.at[slot], leaf_sems.at[slot]
        ).wait()

        @pl.when(slot < live)
        def _():
            spread(mid_cov, closed_leaf.at[slot], noise_cov, moved, leaf_cov.at[slot])

        @pl.when(slot >= live)
        def _():
            leaf_cov[slot, :, :] = jnp.zeros((NX, NX), bf16)

        pltpu.make_async_copy(
            leaf_cov.at[slot], leaf_cov_out.at[slot], leaf_out_sems.at[slot]
        ).start()

    for copy in leaving:
        copy.wait()

    @pl.loop(0, slots)
    def _(slot):
        pltpu.make_async_copy(
            leaf_cov.at[slot], leaf_cov_out.at[slot], leaf_out_sems.at[slot]
        ).wait()


SMEM = pl.BlockSpec(memory_space=pltpu.SMEM)
VMEM = pl.BlockSpec(memory_space=pltpu.VMEM)
HBM = pl.BlockSpec(memory_space=pltpu.HBM)
DMA = pltpu.SemaphoreType.DMA


def limit(mib):
    return pltpu.CompilerParams(vmem_limit_bytes=mib << 20)


COST = pl.CostEstimate(flops=5 * 10**9, bytes_accessed=1 << 18, transcendentals=0)


def matrix(*shape, kind=bf16):
    return jax.ShapeDtypeStruct(shape, kind)


SQUARES = [pltpu.VMEM((T, T), f32)] * 4
PACKED = tuple(matrix(2, rows, T) for rows in ROWS)


def solve(by_core, chunk, control_rows):
    square = matrix(T, T, kind=f32)
    return pl.pallas_call(
        functools.partial(solve_kernel, by_core),
        out_shape=(square, square, square, matrix(HT, T, kind=f32)),
        in_specs=[VMEM] * 3,
        out_specs=(VMEM,) * 4,
        scratch_shapes=[pltpu.VMEM((T, T), f32)],
        compiler_params=limit(8),
        cost_estimate=COST,
        name="solve",
    )(*chunk, control_rows)


def local(
    n_row,
    n_col,
    leaf_state_map,
    leaf_input_map,
    leaf_weight,
    leaf_count,
    mid_state_map,
    mid_input_map,
    mid_weight,
    mid_parent,
    up_state_map,
    up_input_map,
    up_weight,
    root_cov,
    state_cost,
    control_cost,
    noise_cov,
):
    slots = leaf_state_map.shape[0]
    _, core, _ = place_in_col()
    state_rows = state_cost.reshape(NX // T, T)
    control_rows = control_cost.reshape(NU // T, T)
    noise_rows = noise_cov.reshape(NX // T, T)

    mid_gain, mid_value, *packed = pl.pallas_call(
        lower_kernel,
        out_shape=(matrix(NU, NX), matrix(NX, NX), *PACKED),
        in_specs=[SMEM] * 3 + [VMEM] + [HBM] * 4 + [VMEM] * 2,
        out_specs=(VMEM,) * 4,
        scratch_shapes=[
            pltpu.VMEM((slots, NX, NX), bf16),
            pltpu.VMEM((slots, NX, NU), bf16),
            pltpu.VMEM((NX, NX), bf16),
            pltpu.VMEM((NX, NU), bf16),
            DMA((slots,)),
            DMA((slots,)),
            DMA((2,)),
            pltpu.VMEM((NX, T), f32),
            pltpu.VMEM((NX, NX + NU), bf16),
            pltpu.VMEM((NU, NX + NU), f32),
            pltpu.VMEM((NU, NX), f32),
            pltpu.VMEM((NU, NU), f32),
            *SQUARES,
        ],
        compiler_params=pltpu.CompilerParams(vmem_limit_bytes=67043328),
        name="lower",
    )(
        leaf_count,
        mid_weight,
        mid_parent,
        leaf_weight.reshape(1, slots),
        leaf_state_map,
        leaf_input_map,
        mid_state_map,
        mid_input_map,
        state_rows,
        control_rows,
    )
    def across(x, flip):
        return lax.ppermute(x, "col", [(i, i ^ flip) for i in range(n_col)])

    def local_sum(x):
        part = matrix(*x.shape[1:])
        return pl.pallas_call(
            local_sum_kernel,
            out_shape=(part, part),
            in_specs=[SMEM, VMEM, VMEM],
            out_specs=(VMEM, VMEM),
            compiler_params=limit(8),
            name="local_sum",
        )(mid_parent, x, across(x, 1))

    def rest_of_col(kept):
        flip = 4
        while flip < n_col:
            kept = kept + across(kept, flip)
            flip = flip * 2
        return kept, across(kept, 2)

    (kept1, sent1), (kept2, sent2) = (local_sum(x) for x in packed)
    came1 = across(sent1, 2)
    came2 = across(sent2, 2)
    came2, gain_then = lax.optimization_barrier((came2, mid_gain))
    closed_leaf = pl.pallas_call(
        close_kernel,
        grid=(slots,),
        out_shape=matrix(slots, NX, NX),
        in_specs=[
            pl.BlockSpec((None, NX, NX), lambda n: (n, 0, 0)),
            pl.BlockSpec((None, NX, NU), lambda n: (n, 0, 0)),
            VMEM,
        ],
        out_specs=pl.BlockSpec((None, NX, NX), lambda n: (n, 0, 0)),
        compiler_params=limit(16),
        cost_estimate=pl.CostEstimate(
            flops=2 * slots * NX * NX * NU, bytes_accessed=slots * NX * 5 * NU * 2, transcendentals=0
        ),
        name="close",
    )(leaf_state_map, leaf_input_map, gain_then)
    first = rest_of_col(kept1 + came1)
    second = rest_of_col(kept2 + came2)
    solved = solve(False, first, control_rows)
    up_weight, closed_leaf = lax.optimization_barrier((up_weight, closed_leaf))

    up_gain_own, up_value_own, packed = pl.pallas_call(
        upper_kernel,
        out_shape=(matrix(NU, NX), matrix(NX, NX), matrix(2, sum(ROWS), T)),
        in_specs=[SMEM] + [VMEM] * 8 + [HBM] * 2 + [VMEM],
        out_specs=(VMEM,) * 3,
        scratch_shapes=[
            pltpu.VMEM((NX, NX), bf16),
            pltpu.VMEM((NX, NU), bf16),
            DMA((2,)),
            pltpu.VMEM((NX, NX + NU), bf16),
        ],
        compiler_params=limit(24),
        name="upper",
    )(up_weight, *first, *second, *solved, up_state_map, up_input_map, state_rows)
    up_gain_other = across(up_gain_own, 1)
    up_value_other = across(up_value_own, 1)

    row_bits = n_row.bit_length() - 1
    is_low = core == 0

    def along(x, step):
        bits = (step % row_bits, (step + row_bits // 2) % row_bits)
        return lax.ppermute(
            x,
            ("row", "col"),
            [
                (r * n_col + c, (r ^ (1 << bits[c % 2])) * n_col + c)
                for r in range(n_row)
                for c in range(n_col)
            ],
        )

    kept = jnp.where(is_low, packed[0], packed[1]) + across(
        jnp.where(is_low, packed[1], packed[0]), 1
    )
    for step in range(row_bits):
        kept = kept + along(kept, step)

    root_gain, root_value, up_gain, up_value, up_cov, mid_cov, leaf_cov = pl.pallas_call(
        root_kernel,
        out_shape=(
            matrix(NU, NX),
            matrix(NX, NX),
            matrix(S1_ROW, NU, NX),
            matrix(S1_ROW, NX, NX),
            matrix(S1_ROW, NX, NX),
            matrix(1, NX, NX),
            matrix(slots, NX, NX),
        ),
        in_specs=[SMEM] * 2 + [VMEM] * 9 + [HBM] * 6,
        out_specs=(HBM,) * 7,
        scratch_shapes=[
            pltpu.VMEM((NU, NX), bf16),
            pltpu.VMEM((NX, NX), bf16),
            pltpu.VMEM((NX, NX), bf16),
            pltpu.VMEM((S1_ROW, NX, NX), bf16),
            pltpu.VMEM((S1_ROW, NX, NU), bf16),
            pltpu.VMEM((NX, NX), bf16),
            pltpu.VMEM((NX, NU), bf16),
            pltpu.VMEM((slots, NX, NX), bf16),
            pltpu.VMEM((NU, NX), bf16),
            pltpu.VMEM((S1_ROW, NX, NX), bf16),
            pltpu.VMEM((NX, NX), bf16),
            pltpu.VMEM((slots, NX, NX), bf16),
            pltpu.VMEM((NX, NX), bf16),
            pltpu.VMEM((NX, NX), bf16),
            DMA((5,)),
            DMA((slots,)),
            DMA((8,)),
            DMA((slots,)),
            *SQUARES,
            pltpu.VMEM((HT, T), f32),
        ],
        compiler_params=limit(32),
        name="root",
    )(
        leaf_count,
        mid_parent,
        kept,
        across(kept, 1),
        state_rows,
        control_rows,
        noise_rows,
        up_gain_own,
        up_gain_other,
        up_value_own,
        up_value_other,
        root_cov,
        up_state_map,
        up_input_map,
        mid_state_map,
        mid_input_map,
        closed_leaf,
    )
    return (
        root_gain,
        root_value,
        up_gain,
        up_value,
        up_cov,
        mid_gain[None],
        mid_value[None],
        mid_cov,
        leaf_cov,
    )


def solution(mesh):
    both = P(("row", "col"), None, None)
    flat = P(("row", "col"))
    up = P("row", None, None)
    return jax.shard_map(
        functools.partial(local, mesh.shape["row"], mesh.shape["col"]),
        mesh=mesh,
        in_specs=(
            both, both, flat, flat, both, both, flat, flat, up, up, P("row"), P(), P(), P(), P(),
        ),
        out_specs=(P(), P(), up, up, up, both, both, both, both),
        check_vma=False,
    )
```
